128 devices in a mesh: tile: 16 (over y, x_lo, core), head: 8 (over x_hi, z).
Axes of the slice: x: 4 (x_hi: 2, x_lo: 2; x = x_hi * 2 + x_lo), y: 4, z: 4, core: 2. Of those that a mesh axis runs over, the one named last changes fastest.
Arguments:
- cells: bfloat16 [16, 12, 640, 1024], P('tile', None, None, 'head'), may hold values from -8 to 8
- conv_weight: float32 [9, 1024], P(None, 'head'), may hold values from -2 to 2
- qkv_weight: bfloat16 [3, 1024, 1024], P(None, None, 'head'), may hold values from -0.1875 to 0.1875
- out_weight: bfloat16 [1024, 1024], P(None, 'head'), may hold values from -0.1875 to 0.1875
- block_mask: int32 [6, 20], replicated, may hold values 0 or 1
Outputs:
- result: bfloat16 [16, 12, 640, 1024], P('tile', None, None, 'head')
The draws below stay inside these ranges and needn't reach their ends.
All inputs are finite; a program needn't handle non-finite values.
Results may differ from the reference program's by a relative error of at most 0.012.
The reference program's roundings to bfloat16 on the way count: a program that leaves them out, or rounds other values in their place, can miss the bound.
Values may be sent and summed in bfloat16 or wider, within the bound.
A program may use at most 128 MiB of HBM per device.

```python
import jax
import jax.numpy as jnp
from jax import lax

D = 1024
HEADS = 16
HEAD_DIM = 64
WIN = 7
TILE = 32
COLS = 640
BR = 12
RADIUS = 3
NR = 192


def draw_cells(key, part):
    base = jax.random.normal(key, (NR // BR, BR, COLS, D), jnp.float32)
    return jnp.clip(base, -8.0, 8.0).astype(jnp.bfloat16)


def touch_ends(values, rng, low, high):
    dims = values.shape
    index_at = [jax.random.randint(jax.random.fold_in(rng, axis), (), 0, dims[axis]) for axis in range(len(dims))]
    values = values.at[tuple(index_at)].set(low)
    longest = dims.index(max(dims))
    index_at[longest] = (index_at[longest] + 1) % dims[longest]
    return values.at[tuple(index_at)].set(high)


def block_scale(own_key, shape, pieces, least, high):
    def one(dim, parts):
        draws = jax.random.uniform(jax.random.fold_in(jax.random.fold_in(own_key, 6), dim), (parts,), jnp.float32, least / len(pieces), high / len(pieces))
        return jnp.repeat(jnp.exp(draws), shape[dim] // parts).reshape((-1,) + (1,) * (len(shape) - dim - 1))

    loudness = one(*pieces[0])
    for cut in pieces[1:]:
        loudness = loudness * one(*cut)
    return loudness


def scatter_about(own_key, shape, width, limit, pieces=(), kind=jnp.bfloat16):
    entries = jax.random.normal(own_key, shape, jnp.float32) * width
    if len(pieces) > 0:
        entries = block_scale(own_key, shape, pieces, -0.22, 0.18) * entries
    return jnp.clip(entries, min=-limit, max=limit).astype(kind)


def setup_inputs(seed: int = 0) -> dict:
    seeds = jax.random.split(jax.random.key(seed), 6)
    return {
        "cells": draw_cells(jax.random.fold_in(seeds[5], 71), 0),
        "conv_weight": scatter_about(seeds[1], (9, D), 0.35, 2.0, ((1, 8),), jnp.float32),
        "qkv_weight": scatter_about(seeds[2], (3, D, D), D ** -0.5, 0.1875, ((2, 8),)),
        "out_weight": scatter_about(seeds[3], (D, D), D ** -0.5, 0.1875, ((1, 8),)),
        "block_mask": touch_ends((jax.random.randint(seeds[4], (NR // TILE, COLS // TILE), 0, 4) < 3).astype(jnp.int32), jax.random.fold_in(seeds[4], 1), 0, 1),
    }


def tile_occupancy(block_mask):
    tile_rows = block_mask.shape[0]
    tile_cols = block_mask.shape[1]
    spread = jnp.broadcast_to(block_mask[:, None, :, None], (tile_rows, TILE, tile_cols, TILE))
    return spread.reshape(tile_rows * TILE, tile_cols * TILE)


def reference(cells, conv_weight, qkv_weight, out_weight, block_mask):
    slab = cells.reshape(NR, COLS, D)
    values = slab.astype(jnp.float32)
    padded = jnp.pad(values, ((1, 1), (1, 1), (0, 0)))
    conv_sum = jnp.zeros_like(values)
    for row_off in range(3):
        for col_off in range(3):
            conv_sum = conv_sum + conv_weight[3 * row_off + col_off] * padded[row_off:row_off + NR, col_off:col_off + COLS]
    mixed = (values + conv_sum).astype(jnp.bfloat16)
    flat_cells = mixed.reshape(NR * COLS, D)
    projected = []
    for which in range(3):
        part_out = jnp.dot(flat_cells, qkv_weight[which], preferred_element_type=jnp.float32).astype(jnp.bfloat16)
        projected.append(jnp.transpose(part_out.reshape(NR, COLS, HEADS, HEAD_DIM), (2, 0, 1, 3)))
    occupancy = jnp.pad(tile_occupancy(block_mask), RADIUS)
    score_scale = HEAD_DIM ** -0.5

    def one_head(triple):
        query_head, key_head, value_head = triple
        key_pad = jnp.pad(key_head, ((RADIUS, RADIUS), (RADIUS, RADIUS), (0, 0)))
        value_pad = jnp.pad(value_head, ((RADIUS, RADIUS), (RADIUS, RADIUS), (0, 0)))
        query_wide = query_head.astype(jnp.float32)
        score_list = []
        allowed_list = []
        for row_off in range(WIN):
            for col_off in range(WIN):
                shifted = key_pad[row_off:row_off + NR, col_off:col_off + COLS].astype(jnp.float32)
                score_list.append(jnp.sum(query_wide * shifted, axis=-1) * score_scale)
                if row_off == RADIUS and col_off == RADIUS:
                    allowed_list.append(jnp.ones((NR, COLS), dtype=bool))
                else:
                    allowed_list.append(occupancy[row_off:row_off + NR, col_off:col_off + COLS] > 0)
        scores = jnp.stack(score_list)
        allowed = jnp.stack(allowed_list)
        masked = jnp.where(allowed, scores, jnp.float32(-1e30))
        row_peak = jnp.max(masked, axis=0)
        exp_scores = jnp.exp(masked - row_peak)
        weights = (exp_scores / jnp.sum(exp_scores, axis=0)).astype(jnp.bfloat16)
        running = jnp.zeros((NR, COLS, HEAD_DIM), jnp.float32)
        for row_off in range(WIN):
            for col_off in range(WIN):
                position = row_off * WIN + col_off
                shifted = value_pad[row_off:row_off + NR, col_off:col_off + COLS].astype(jnp.float32)
                running = running + weights[position].astype(jnp.float32)[:, :, None] * shifted
        return running.astype(jnp.bfloat16)

    attended = lax.map(one_head, (projected[0], projected[1], projected[2]))
    attended = jnp.transpose(attended, (1, 2, 0, 3)).reshape(NR * COLS, D)
    final_proj = jnp.dot(attended, out_weight, preferred_element_type=jnp.float32).reshape(NR, COLS, D)
    final = (values + final_proj).astype(jnp.bfloat16)
    return final.reshape(NR // BR, BR, COLS, D)
```

```python
import functools
import math

import jax
import jax.numpy as jnp
from jax import lax
from jax.experimental import pallas as pl
from jax.experimental.pallas import tpu as pltpu
from jax.sharding import PartitionSpec as P

MESH = pl.DeviceIdType.MESH
NT = 16
NH = 8
ROWS = 12
COLS = 640
CW = 80
WC = 96
BC = 112
CH = 128
D = 1024
TILE = 32
WROWS = ROWS + 8
KROWS = ROWS + 6
SLAB = 128
NEG = -1e30
EXP_SCALE = math.log2(math.e) / 8.0


def kernel(
    cells, conv_w, wqkv, wout, bmask, out,
    win, w4, cw, mixed, qbuf, kbuf, vbuf, att, ob,
    loc_sem, w_s, w_r, o_s, o_r, c_s, c_r, m_s, m_r, u_s, u_r, d_s, d_r,
    y_s, y_r, r_s, r_r, rl_s,
):
    t = lax.axis_index("tile")
    h = lax.axis_index("head")
    yrow = t // 4
    core = t % 2
    low = (t // 2) % 2
    y_up = (t + 4) % NT
    y_dn = (t + 12) % NT
    sib = t + 1 - 2 * core
    not_top = t > 0
    not_bot = t < NT - 1

    def slab_row(yy, cc):
        return pl.multiple_of(SLAB * (2 * yy + cc), SLAB)

    @pl.when(t == 0)
    def _():
        win[:, 0:4] = jnp.zeros((NH, 4, BC, CH), jnp.bfloat16)

    @pl.when(t == NT - 1)
    def _():
        win[:, 16:20] = jnp.zeros((NH, 4, BC, CH), jnp.bfloat16)

    @pl.when(h == 0)
    def _():
        win[:, :, 0:16] = jnp.zeros((NH, WROWS, 16, CH), jnp.bfloat16)

    @pl.when(h == NH - 1)
    def _():
        win[:, :, 96:112] = jnp.zeros((NH, WROWS, 16, CH), jnp.bfloat16)

    bar = pltpu.get_barrier_semaphore()
    for k in range(1, NH):
        pl.semaphore_signal(bar, inc=1, device_id=(t, (h + k) % NH), device_id_type=MESH)
    for other in (y_up, y_dn):
        pl.semaphore_signal(bar, inc=1, device_id=(other, h), device_id_type=MESH)

    @pl.when(not_top)
    def _():
        for k in range(NH):
            pl.semaphore_signal(bar, inc=1, device_id=(t - 1, (h + k) % NH), device_id_type=MESH)

    @pl.when(not_bot)
    def _():
        for k in range(NH):
            pl.semaphore_signal(bar, inc=1, device_id=(t + 1, (h + k) % NH), device_id_type=MESH)

    bands_near = jnp.where(not_top, 1, 0) + jnp.where(not_bot, 1, 0)
    pl.semaphore_wait(bar, NH + 1 + NH * bands_near)

    def win_start(hd):
        return pl.multiple_of(jnp.clip(CW * hd - 8, 0, COLS - WC), 8)

    def win_at(hd):
        return pl.multiple_of(win_start(hd) - CW * hd + 16, 8)

    own_rows = slab_row(yrow, core)

    def w_copy(k, hs, ht):
        return pltpu.make_async_remote_copy(
            src_ref=wqkv.at[:, pl.ds(own_rows, SLAB), :],
            dst_ref=w4.at[0:3, pl.ds(own_rows, SLAB), pl.ds(pl.multiple_of(CH * hs, CH), CH)],
            send_sem=w_s.at[k], recv_sem=w_r.at[k],
            device_id=(t, ht), device_id_type=MESH)

    def o_copy(k, hs, ht):
        return pltpu.make_async_remote_copy(
            src_ref=wout.at[pl.ds(own_rows, SLAB), :],
            dst_ref=w4.at[3, pl.ds(own_rows, SLAB), pl.ds(pl.multiple_of(CH * hs, CH), CH)],
            send_sem=o_s.at[k], recv_sem=o_r.at[k],
            device_id=(t, ht), device_id_type=MESH)

    def c_copy(k, hs, ht):
        return pltpu.make_async_remote_copy(
            src_ref=conv_w, dst_ref=cw.at[hs],
            send_sem=c_s.at[k], recv_sem=c_r.at[k],
            device_id=(t, ht), device_id_type=MESH)

    def m_copy(k, hs, ht):
        return pltpu.make_async_remote_copy(
            src_ref=cells.at[0, :, pl.ds(win_start(ht), WC), :],
            dst_ref=win.at[hs, 4:16, pl.ds(win_at(ht), WC), :],
            send_sem=m_s.at[k], recv_sem=m_r.at[k],
            device_id=(t, ht), device_id_type=MESH)

    def u_copy(k, hs, ht):
        return pltpu.make_async_remote_copy(
            src_ref=cells.at[0, 0:4, pl.ds(win_start(ht), WC), :],
            dst_ref=win.at[hs, 16:20, pl.ds(win_at(ht), WC), :],
            send_sem=u_s.at[k], recv_sem=u_r.at[k],
            device_id=(t - 1, ht), device_id_type=MESH)

    def d_copy(k, hs, ht):
        return pltpu.make_async_remote_copy(
            src_ref=cells.at[0, 8:12, pl.ds(win_start(ht), WC), :],
            dst_ref=win.at[hs, 0:4, pl.ds(win_at(ht), WC), :],
            send_sem=d_s.at[k], recv_sem=d_r.at[k],
            device_id=(t + 1, ht), device_id_type=MESH)

    local = [
        pltpu.make_async_copy(
            wqkv.at[:, pl.ds(own_rows, SLAB), :],
            w4.at[0:3, pl.ds(own_rows, SLAB), pl.ds(pl.multiple_of(CH * h, CH), CH)], loc_sem.at[0]),
        pltpu.make_async_copy(
            wout.at[pl.ds(own_rows, SLAB), :],
            w4.at[3, pl.ds(own_rows, SLAB), pl.ds(pl.multiple_of(CH * h, CH), CH)], loc_sem.at[1]),
        pltpu.make_async_copy(conv_w, cw.at[h], loc_sem.at[2]),
        pltpu.make_async_copy(
            cells.at[0, :, pl.ds(win_start(h), WC), :],
            win.at[h, 4:16, pl.ds(win_at(h), WC), :], loc_sem.at[3]),
    ]
    for k in range(1, NH):
        ht = (h + k) % NH
        w_copy(k, h, ht).start()
        o_copy(k, h, ht).start()
    for cp in local:
        cp.start()
    for k in range(1, NH):
        c_copy(k, h, (h + k) % NH).start()
    for k in range(NH):
        ht = (h + k) % NH
        if k:
            m_copy(k, h, ht).start()

        @pl.when(not_top)
        def _():
            u_copy(k, h, ht).start()

        @pl.when(not_bot)
        def _():
            d_copy(k, h, ht).start()

    def y_copy(idx, yy, cc, to, first=0, size=SLAB):
        rows = pl.ds(pl.multiple_of(slab_row(yy, cc) + first, size), size)
        return pltpu.make_async_remote_copy(
            src_ref=w4.at[:, rows, :], dst_ref=w4.at[:, rows, :],
            send_sem=y_s.at[idx], recv_sem=y_r.at[idx],
            device_id=(to, h), device_id_type=MESH)

    y1 = (yrow + 3) % 4
    y2 = (yrow + 2) % 4
    y3 = (yrow + 1) % 4
    other = 1 - core
    half = SLAB // 2

    local[0].wait()
    local[1].wait()
    for k in range(1, NH):
        hs = (h + NH - k) % NH
        w_copy(k, hs, h).wait_recv()
        o_copy(k, hs, h).wait_recv()
    y_copy(0, yrow, core, y_up).start()
    y_copy(1, yrow, core, y_dn).start()
    y_copy(2, yrow, core, sib).start()

    y_copy(0, y1, core, y_up).wait_recv()
    y_copy(3, y1, core, y_up, 0, half).start()
    y_copy(5, y1, core, sib).start()
    y_copy(1, y3, core, y_dn).wait_recv()
    y_copy(4, y3, core, y_dn, half, half).start()
    y_copy(6, y3, core, sib).start()

    local[2].wait()
    local[3].wait()

    def conv_chunk(k, carry):
        hs = (h + NH - k) % NH

        @pl.when(k > 0)
        def _():
            c_copy(k, hs, h).wait_recv()
            m_copy(k, hs, h).wait_recv()

        @pl.when(not_bot)
        def _():
            u_copy(k, hs, h).wait_recv()

        @pl.when(not_top)
        def _():
            d_copy(k, hs, h).wait_recv()

        taps = [jnp.broadcast_to(cw[hs, pl.ds(i, 1), :], (WC, CH)) for i in range(9)]
        lanes = pl.ds(pl.multiple_of(CH * hs, CH), CH)

        def row(i):
            return win[hs, i].astype(jnp.float32)[8:104]

        rows = [row(0), row(1), None]
        for r in range(KROWS):
            rows[2] = row(r + 2)
            side = []
            for b in range(3):
                acc = taps[b] * rows[0]
                acc = acc + taps[3 + b] * rows[1]
                acc = acc + taps[6 + b] * rows[2]
                side.append(acc)
            conv = pltpu.roll(side[0], 1, 0) + side[1] + pltpu.roll(side[2], WC - 1, 0)
            mixed[pl.ds(WC * r, WC), lanes] = (rows[1] + conv).astype(jnp.bfloat16)
            rows = [rows[1], rows[2], None]
        return carry

    lax.fori_loop(0, 4, conv_chunk, 0)

    y_copy(3, y2, core, y_up, 0, half).wait_recv()
    y_copy(4, y2, core, y_dn, half, half).wait_recv()
    y_copy(7, y2, core, sib).start()

    lax.fori_loop(4, NH, conv_chunk, 0)

    y_copy(2, yrow, other, sib).wait_recv()
    y_copy(5, y1, other, sib).wait_recv()
    y_copy(6, y3, other, sib).wait_recv()
    y_copy(7, y2, other, sib).wait_recv()

    BLK = 3 * WC

    def kv_block(i, carry):
        def part(n, c2):
            lanes = pl.ds(pl.multiple_of(256 * n, 256), 256)
            x = mixed[pl.ds(pl.multiple_of(BLK * i, BLK), BLK), :]
            for plane, ref in ((1, kbuf), (2, vbuf)):
                y = jnp.dot(x, w4[plane, :, lanes], preferred_element_type=jnp.float32)
                ref[pl.ds(3 * i, 3), :, lanes] = y.astype(jnp.bfloat16).reshape(3, WC, 256)
            return c2

        return lax.fori_loop(0, 4, part, carry)

    def q_block(i, carry):
        def part(n, c2):
            lanes = pl.ds(pl.multiple_of(256 * n, 256), 256)
            x = mixed[pl.ds(pl.multiple_of(BLK * (i + 1), BLK), BLK), :]
            y = jnp.dot(x, w4[0, :, lanes], preferred_element_type=jnp.float32)
            y = y.reshape(3, WC, 256)[:, 8:88]
            qbuf[pl.ds(3 * i, 3), :, lanes] = y.astype(jnp.bfloat16)
            return c2

        return lax.fori_loop(0, 4, part, carry)

    lax.fori_loop(0, 6, kv_block, 0)
    lax.fori_loop(0, 4, q_block, 0)

    qi = lax.broadcasted_iota(jnp.int32, (32, 256), 0)
    ki = lax.broadcasted_iota(jnp.int32, (32, 256), 1)
    drow = ki // 32 - qi // 16 - 3
    dcol = ki % 32 - qi % 16 - 8
    band = (drow >= -3) & (drow <= 3) & (dcol >= -3) & (dcol <= 3)
    self_bias = jnp.where((drow == 0) & (dcol == 0), 0.0, NEG).astype(jnp.float32)
    band_f = jnp.where(band, 1.0, 0.0).astype(jnp.float32)
    lane1 = lax.broadcasted_iota(jnp.int32, (1, 256), 1)
    head_of = lax.broadcasted_iota(jnp.int32, (32, 256), 1) // 64
    head_on = [jnp.where(head_of == i, 1.0, 0.0).astype(jnp.bfloat16) for i in range(4)]

    def occ_at(rt, ct):
        inside = (rt >= 0) & (rt < 6) & (ct >= 0) & (ct < 20)
        value = bmask[jnp.clip(rt, 0, 5), jnp.clip(ct, 0, 19)]
        return jnp.where(inside, value, 0)

    def r_copy(i, k, hs, ht):
        return pltpu.make_async_remote_copy(
            src_ref=ob.at[ht, pl.ds(2 * i, 2)],
            dst_ref=out.at[0, pl.ds(2 * i, 2), pl.ds(pl.multiple_of(CW * hs, 16), CW), :],
            send_sem=r_s.at[i, k], recv_sem=r_r.at[i, k],
            device_id=(t, ht), device_id_type=MESH)

    def r_local(i):
        return pltpu.make_async_copy(
            ob.at[h, pl.ds(2 * i, 2)],
            out.at[0, pl.ds(2 * i, 2), pl.ds(pl.multiple_of(CW * h, 16), CW), :],
            rl_s.at[i])

    def row_pair(i, carry):
        r0 = 2 * i

        def col_tile(j, c2):
            row0 = ROWS * t - 3 + r0
            col0 = CW * h - 8 + 16 * j
            rt = (row0 + 32) // 32 - 1
            ct = (col0 + 32) // 32 - 1
            in_r = (row0 + lane1 // 32 + 32) // 32 - 1 == rt
            in_c = (col0 + lane1 % 32 + 32) // 32 - 1 == ct
            occ = jnp.where(
                in_r,
                jnp.where(in_c, occ_at(rt, ct), occ_at(rt, ct + 1)),
                jnp.where(in_c, occ_at(rt + 1, ct), occ_at(rt + 1, ct + 1)))
            occ_f = occ.astype(jnp.float32)
            bias = jnp.where(band_f * occ_f > 0.5, 0.0, self_bias)
            cols = pl.ds(pl.multiple_of(16 * j, 16), 16)
            kcols = pl.ds(pl.multiple_of(16 * j, 16), 32)
            for g in range(4):
                lanes = slice(256 * g, 256 * g + 256)
                q = qbuf[pl.ds(r0, 2), cols, lanes].reshape(32, 256)
                kk = kbuf[pl.ds(r0, 8), kcols, lanes].reshape(256, 256)
                vv = vbuf[pl.ds(r0, 8), kcols, lanes].reshape(256, 256)
                q4 = jnp.concatenate([q * head_on[n] for n in range(4)], axis=0)
                s = lax.dot_general(q4, kk, (((1,), (1,)), ((), ())),
                                    preferred_element_type=jnp.float32)
                s = s.reshape(4, 32, 256) + bias[None]
                peak = jnp.max(s, axis=-1, keepdims=True)
                e = jnp.exp2((s - peak) * EXP_SCALE)
                total = jnp.sum(e, axis=-1, keepdims=True)
                p = (e * (1.0 / total)).astype(jnp.bfloat16).reshape(128, 256)
                o = jnp.dot(p, vv, preferred_element_type=jnp.float32)
                o = jnp.where(
                    head_of == 0, o[0:32],
                    jnp.where(head_of == 1, o[32:64],
                              jnp.where(head_of == 2, o[64:96], o[96:128])))
                att[:, cols, lanes] = o.astype(jnp.bfloat16).reshape(2, 16, 256)
            return c2

        lax.fori_loop(0, 5, col_tile, 0)

        x = att[...].reshape(2 * CW, D)
        for n in range(4):
            y = jnp.dot(x, w4[3, :, 256 * n:256 * n + 256], preferred_element_type=jnp.float32)
            for m in range(2):
                dst = 2 * n + m
                slab = win[dst, pl.ds(4 + r0, 2), 16:96, :].astype(jnp.float32)
                res = slab + y[:, CH * m:CH * m + CH].reshape(2, CW, CH)
                ob[dst, pl.ds(r0, 2)] = res.astype(jnp.bfloat16)
        r_local(i).start()
        for k in range(1, NH):
            r_copy(i, k, h, (h + k) % NH).start()
        return carry

    lax.fori_loop(0, ROWS // 2, row_pair, 0)

    def drain(i, carry):
        r_local(i).wait()
        for k in range(1, NH):
            r_copy(i, k, h, (h + k) % NH).wait_send()
            r_copy(i, k, (h + NH - k) % NH, h).wait_recv()
        return carry

    for k in range(1, NH):
        ht = (h + k) % NH
        w_copy(k, h, ht).wait_send()
        o_copy(k, h, ht).wait_send()
        c_copy(k, h, ht).wait_send()
        m_copy(k, h, ht).wait_send()
    for k in range(NH):
        ht = (h + k) % NH

        @pl.when(not_top)
        def _():
            u_copy(k, h, ht).wait_send()

        @pl.when(not_bot)
        def _():
            d_copy(k, h, ht).wait_send()
    y_copy(0, yrow, core, y_up).wait_send()
    y_copy(1, yrow, core, y_dn).wait_send()
    y_copy(2, yrow, core, sib).wait_send()
    y_copy(3, y1, core, y_up, 0, half).wait_send()
    y_copy(4, y3, core, y_dn, half, half).wait_send()
    y_copy(5, y1, core, sib).wait_send()
    y_copy(6, y3, core, sib).wait_send()
    y_copy(7, y2, core, sib).wait_send()
    lax.fori_loop(0, ROWS // 2, drain, 0)


def per_device(cells, conv_weight, qkv_weight, out_weight, block_mask):
    hbm = pl.BlockSpec(memory_space=pl.ANY)
    bf = jnp.bfloat16
    sem = pltpu.SemaphoreType.DMA
    pairs = ROWS // 2
    return pl.pallas_call(
        kernel,
        out_shape=jax.ShapeDtypeStruct((1, ROWS, COLS, CH), bf),
        in_specs=[hbm, hbm, hbm, hbm, pl.BlockSpec(memory_space=pltpu.SMEM)],
        out_specs=hbm,
        scratch_shapes=[
            pltpu.VMEM((NH, WROWS, BC, CH), bf),
            pltpu.VMEM((4, D, D), bf),
            pltpu.VMEM((NH, 9, CH), jnp.float32),
            pltpu.VMEM((KROWS * WC, D), bf),
            pltpu.VMEM((ROWS, CW, D), bf),
            pltpu.VMEM((KROWS, WC, D), bf),
            pltpu.VMEM((KROWS, WC, D), bf),
            pltpu.VMEM((2, CW, D), bf),
            pltpu.VMEM((NH, ROWS, CW, CH), bf),
            sem((4,)),
            sem((NH,)), sem((NH,)), sem((NH,)), sem((NH,)), sem((NH,)), sem((NH,)),
            sem((NH,)), sem((NH,)), sem((NH,)), sem((NH,)), sem((NH,)), sem((NH,)),
            sem((8,)), sem((8,)),
            sem((pairs, NH)), sem((pairs, NH)), sem((pairs,)),
        ],
        compiler_params=pltpu.CompilerParams(
            collective_id=0, has_side_effects=True, vmem_limit_bytes=56 * 1024 * 1024),
        name="band_layer",
    )(cells, conv_weight, qkv_weight, out_weight, block_mask)


def solution(mesh):
    placed = (
        P("tile", None, None, "head"),
        P(None, "head"),
        P(None, None, "head"),
        P(None, "head"),
        P(),
    )
    return jax.shard_map(
        per_device,
        mesh=mesh,
        in_specs=placed,
        out_specs=P("tile", None, None, "head"),
        check_vma=False,
    )
```

```python
import functools
import math

import jax
import jax.numpy as jnp
from jax import lax
from jax.experimental import pallas as pl
from jax.experimental.pallas import tpu as pltpu
from jax.sharding import PartitionSpec as P

MESH = pl.DeviceIdType.MESH
NT = 16
NH = 8
ROWS = 12
COLS = 640
CW = 80
WC = 96
BC = 112
CH = 128
D = 1024
TILE = 32
WROWS = ROWS + 8
KROWS = ROWS + 6
SLAB = 128
AHEAD = 2
EARLY = 3
NEG = -1e30
EXP_SCALE = math.log2(math.e) / 8.0


def kernel(
    cells, conv_w, wqkv, wout, bmask, out,
    win, w4, cw, mixed, qbuf, kbuf, vbuf, att, ob,
    loc_sem, w_s, w_r, o_s, o_r, c_s, c_r, m_s, m_r, u_s, u_r, d_s, d_r,
    y_s, y_r, r_s, r_r, rl_s,
):
    t = lax.axis_index("tile")
    h = lax.axis_index("head")
    yrow = t // 4
    core = t % 2
    low = (t // 2) % 2
    y_up = (t + 4) % NT
    y_dn = (t + 12) % NT
    sib = t + 1 - 2 * core
    flip = 2 - 4 * low
    not_top = t > 0
    not_bot = t < NT - 1

    def slab_row(yy, cc):
        return pl.multiple_of(SLAB * (2 * yy + cc), SLAB)

    @pl.when(t == 0)
    def _():
        win[:, 0:4] = jnp.zeros((NH, 4, BC, CH), jnp.bfloat16)

    @pl.when(t == NT - 1)
    def _():
        win[:, 16:20] = jnp.zeros((NH, 4, BC, CH), jnp.bfloat16)

    @pl.when(h == 0)
    def _():
        win[:, :, 0:16] = jnp.zeros((NH, WROWS, 16, CH), jnp.bfloat16)

    @pl.when(h == NH - 1)
    def _():
        win[:, :, 96:112] = jnp.zeros((NH, WROWS, 16, CH), jnp.bfloat16)

    bar = pltpu.get_barrier_semaphore()
    for k in range(1, NH):
        pl.semaphore_signal(bar, inc=1, device_id=(t, (h + k) % NH), device_id_type=MESH)
    for other in (y_up, y_dn):
        pl.semaphore_signal(bar, inc=1, device_id=(other, h), device_id_type=MESH)
    for z in range(4):
        far = 4 * (1 - h // 4) + z
        pl.semaphore_signal(bar, inc=1, device_id=(t + flip, far), device_id_type=MESH)

    @pl.when(not_top)
    def _():
        pl.semaphore_signal(bar, inc=1, device_id=(t - 1, h), device_id_type=MESH)

    @pl.when(not_bot)
    def _():
        pl.semaphore_signal(bar, inc=1, device_id=(t + 1, h), device_id_type=MESH)

    bands_near = jnp.where(not_top, 1, 0) + jnp.where(not_bot, 1, 0)
    pl.semaphore_wait(bar, NH - 1 + 2 + 4 + bands_near)

    def win_start(hd):
        return pl.multiple_of(jnp.clip(CW * hd - 8, 0, COLS - WC), 8)

    def win_at(hd):
        return pl.multiple_of(win_start(hd) - CW * hd + 16, 8)

    own_rows = slab_row(yrow, core)

    def tile_for(hs, ht):
        return t + flip * ((hs // 4 + ht // 4) % 2)

    def w_copy(k, hs, ht):
        return pltpu.make_async_remote_copy(
            src_ref=wqkv.at[:, pl.ds(own_rows, SLAB), :],
            dst_ref=w4.at[0:3, pl.ds(own_rows, SLAB), pl.ds(pl.multiple_of(CH * hs, CH), CH)],
            send_sem=w_s.at[k], recv_sem=w_r.at[k],
            device_id=(tile_for(hs, ht), ht), device_id_type=MESH)

    def o_copy(k, hs, ht):
        return pltpu.make_async_remote_copy(
            src_ref=wout.at[pl.ds(own_rows, SLAB), :],
            dst_ref=w4.at[3, pl.ds(own_rows, SLAB), pl.ds(pl.multiple_of(CH * hs, CH), CH)],
            send_sem=o_s.at[k], recv_sem=o_r.at[k],
            device_id=(tile_for(hs, ht), ht), device_id_type=MESH)

    def c_copy(k, hs, ht):
        return pltpu.make_async_remote_copy(
            src_ref=conv_w, dst_ref=cw.at[hs],
            send_sem=c_s.at[k], recv_sem=c_r.at[k],
            device_id=(t, ht), device_id_type=MESH)

    def m_copy(k, hs, ht):
        return pltpu.make_async_remote_copy(
            src_ref=cells.at[0, :, pl.ds(win_start(ht), WC), :],
            dst_ref=win.at[hs, 4:16, pl.ds(win_at(ht), WC), :],
            send_sem=m_s.at[k], recv_sem=m_r.at[k],
            device_id=(t, ht), device_id_type=MESH)

    own_win = pl.ds(win_at(h), WC)

    def u_copy(k, hs):
        return pltpu.make_async_remote_copy(
            src_ref=win.at[hs, 4:8, own_win, :], dst_ref=win.at[hs, 16:20, own_win, :],
            send_sem=u_s.at[k], recv_sem=u_r.at[k],
            device_id=(t - 1, h), device_id_type=MESH)

    def d_copy(k, hs):
        return pltpu.make_async_remote_copy(
            src_ref=win.at[hs, 12:16, own_win, :], dst_ref=win.at[hs, 0:4, own_win, :],
            send_sem=d_s.at[k], recv_sem=d_r.at[k],
            device_id=(t + 1, h), device_id_type=MESH)

    def pass_on(k):
        hs = (h + NH - k) % NH

        @pl.when(not_top)
        def _():
            u_copy(k, hs).start()

        @pl.when(not_bot)
        def _():
            d_copy(k, hs).start()

    local = [
        pltpu.make_async_copy(
            wqkv.at[:, pl.ds(own_rows, SLAB), :],
            w4.at[0:3, pl.ds(own_rows, SLAB), pl.ds(pl.multiple_of(CH * h, CH), CH)], loc_sem.at[0]),
        pltpu.make_async_copy(
            wout.at[pl.ds(own_rows, SLAB), :],
            w4.at[3, pl.ds(own_rows, SLAB), pl.ds(pl.multiple_of(CH * h, CH), CH)], loc_sem.at[1]),
        pltpu.make_async_copy(conv_w, cw.at[h], loc_sem.at[2]),
        pltpu.make_async_copy(
            cells.at[0, :, pl.ds(win_start(h), WC), :],
            win.at[h, 4:16, pl.ds(win_at(h), WC), :], loc_sem.at[3]),
    ]
    for k in range(1, NH):
        ht = (h + k) % NH
        w_copy(k, h, ht).start()
        o_copy(k, h, ht).start()
    for cp in local:
        cp.start()
    for k in range(1, NH):
        c_copy(k, h, (h + k) % NH).start()
    for k in range(1, NH):
        m_copy(k, h, (h + k) % NH).start()
    local[3].wait()
    pass_on(0)

    def y_copy(idx, yy, cc, to, first=0, size=SLAB):
        rows = pl.ds(pl.multiple_of(slab_row(yy, cc) + first, size), size)
        return pltpu.make_async_remote_copy(
            src_ref=w4.at[:, rows, :], dst_ref=w4.at[:, rows, :],
            send_sem=y_s.at[idx], recv_sem=y_r.at[idx],
            device_id=(to, h), device_id_type=MESH)

    y1 = (yrow + 3) % 4
    y2 = (yrow + 2) % 4
    y3 = (yrow + 1) % 4
    other = 1 - core
    half = SLAB // 2

    local[0].wait()
    local[1].wait()
    for k in range(1, NH):
        hs = (h + NH - k) % NH
        w_copy(k, hs, h).wait_recv()
        o_copy(k, hs, h).wait_recv()
    y_copy(0, yrow, core, y_up).start()
    y_copy(1, yrow, core, y_dn).start()
    y_copy(2, yrow, core, sib).start()

    local[2].wait()
    for k in range(1, AHEAD):
        m_copy(k, (h + NH - k) % NH, h).wait_recv()
        pass_on(k)

    def conv_chunk(k, carry):
        hs = (h + NH - k) % NH

        @pl.when(k + AHEAD < NH)
        def _():
            m_copy(k + AHEAD, (hs + NH - AHEAD) % NH, h).wait_recv()
            pass_on(k + AHEAD)

        @pl.when(k > 0)
        def _():
            c_copy(k, hs, h).wait_recv()

        @pl.when(not_bot)
        def _():
            u_copy(k, hs).wait_recv()

        @pl.when(not_top)
        def _():
            d_copy(k, hs).wait_recv()

        taps = [jnp.broadcast_to(cw[hs, pl.ds(i, 1), :], (WC, CH)) for i in range(9)]
        lanes = pl.ds(pl.multiple_of(CH * hs, CH), CH)

        def row(i):
            return win[hs, i].astype(jnp.float32)[8:104]

        rows = [row(0), row(1), None]
        for r in range(KROWS):
            rows[2] = row(r + 2)
            side = []
            for b in range(3):
                acc = taps[b] * rows[0]
                acc = acc + taps[3 + b] * rows[1]
                acc = acc + taps[6 + b] * rows[2]
                side.append(acc)
            conv = pltpu.roll(side[0], 1, 0) + side[1] + pltpu.roll(side[2], WC - 1, 0)
            mixed[pl.ds(WC * r, WC), lanes] = (rows[1] + conv).astype(jnp.bfloat16)
            rows = [rows[1], rows[2], None]
        return carry

    lax.fori_loop(0, EARLY, conv_chunk, 0)

    y_copy(0, y1, core, y_up).wait_recv()
    y_copy(3, y1, core, y_up, 0, half).start()
    y_copy(5, y1, core, sib).start()
    y_copy(1, y3, core, y_dn).wait_recv()
    y_copy(4, y3, core, y_dn, half, half).start()
    y_copy(6, y3, core, sib).start()

    lax.fori_loop(EARLY, NH, conv_chunk, 0)

    y_copy(3, y2, core, y_up, 0, half).wait_recv()
    y_copy(4, y2, core, y_dn, half, half).wait_recv()
    y_copy(7, y2, core, sib).start()

    y_copy(2, yrow, other, sib).wait_recv()
    y_copy(5, y1, other, sib).wait_recv()
    y_copy(6, y3, other, sib).wait_recv()
    y_copy(7, y2, other, sib).wait_recv()

    BLK = 3 * WC

    def kv_block(i, carry):
        def part(n, c2):
            lanes = pl.ds(pl.multiple_of(256 * n, 256), 256)
            x = mixed[pl.ds(pl.multiple_of(BLK * i, BLK), BLK), :]
            for plane, ref in ((1, kbuf), (2, vbuf)):
                y = jnp.dot(x, w4[plane, :, lanes], preferred_element_type=jnp.float32)
                ref[pl.ds(3 * i, 3), :, lanes] = y.astype(jnp.bfloat16).reshape(3, WC, 256)
            return c2

        return lax.fori_loop(0, 4, part, carry)

    def q_block(i, carry):
        def part(n, c2):
            lanes = pl.ds(pl.multiple_of(256 * n, 256), 256)
            x = mixed[pl.ds(pl.multiple_of(BLK * (i + 1), BLK), BLK), :]
            y = jnp.dot(x, w4[0, :, lanes], preferred_element_type=jnp.float32)
            y = y.reshape(3, WC, 256)[:, 8:88]
            qbuf[pl.ds(3 * i, 3), :, lanes] = y.astype(jnp.bfloat16)
            return c2

        return lax.fori_loop(0, 4, part, carry)

    lax.fori_loop(0, 6, kv_block, 0)
    lax.fori_loop(0, 4, q_block, 0)

    qi = lax.broadcasted_iota(jnp.int32, (32, 256), 0)
    ki = lax.broadcasted_iota(jnp.int32, (32, 256), 1)
    drow = ki // 32 - qi // 16 - 3
    dcol = ki % 32 - qi % 16 - 8
    band = (drow >= -3) & (drow <= 3) & (dcol >= -3) & (dcol <= 3)
    self_bias = jnp.where((drow == 0) & (dcol == 0), 0.0, NEG).astype(jnp.float32)
    band_f = jnp.where(band, 1.0, 0.0).astype(jnp.float32)
    lane1 = lax.broadcasted_iota(jnp.int32, (1, 256), 1)
    head_of = lax.broadcasted_iota(jnp.int32, (32, 256), 1) // 64
    head_on = [jnp.where(head_of == i, 1.0, 0.0).astype(jnp.bfloat16) for i in range(4)]

    def occ_at(rt, ct):
        inside = (rt >= 0) & (rt < 6) & (ct >= 0) & (ct < 20)
        value = bmask[jnp.clip(rt, 0, 5), jnp.clip(ct, 0, 19)]
        return jnp.where(inside, value, 0)

    def r_copy(i, k, hs, ht):
        return pltpu.make_async_remote_copy(
            src_ref=ob.at[ht, pl.ds(2 * i, 2)],
            dst_ref=out.at[0, pl.ds(2 * i, 2), pl.ds(pl.multiple_of(CW * hs, 16), CW), :],
            send_sem=r_s.at[i, k], recv_sem=r_r.at[i, k],
            device_id=(t, ht), device_id_type=MESH)

    def r_local(i):
        return pltpu.make_async_copy(
            ob.at[h, pl.ds(2 * i, 2)],
            out.at[0, pl.ds(2 * i, 2), pl.ds(pl.multiple_of(CW * h, 16), CW), :],
            rl_s.at[i])

    def row_pair(i, carry):
        r0 = 2 * i

        def col_tile(j, c2):
            row0 = ROWS * t - 3 + r0
            col0 = CW * h - 8 + 16 * j
            rt = (row0 + 32) // 32 - 1
            ct = (col0 + 32) // 32 - 1
            in_r = (row0 + lane1 // 32 + 32) // 32 - 1 == rt
            in_c = (col0 + lane1 % 32 + 32) // 32 - 1 == ct
            occ = jnp.where(
                in_r,
                jnp.where(in_c, occ_at(rt, ct), occ_at(rt, ct + 1)),
                jnp.where(in_c, occ_at(rt + 1, ct), occ_at(rt + 1, ct + 1)))
            occ_f = occ.astype(jnp.float32)
            bias = jnp.where(band_f * occ_f > 0.5, 0.0, self_bias)
            cols = pl.ds(pl.multiple_of(16 * j, 16), 16)
            kcols = pl.ds(pl.multiple_of(16 * j, 16), 32)
            scores, probs = [], []
            for g in range(4):
                lanes = slice(256 * g, 256 * g + 256)
                q = qbuf[pl.ds(r0, 2), cols, lanes].reshape(32, 256)
                kk = kbuf[pl.ds(r0, 8), kcols, lanes].reshape(256, 256)
                q4 = jnp.concatenate([q * head_on[n] for n in range(4)], axis=0)
                scores.append(lax.dot_general(q4, kk, (((1,), (1,)), ((), ())),
                                              preferred_element_type=jnp.float32))
            for g in range(4):
                s = scores[g].reshape(4, 32, 256) + bias[None]
                peak = jnp.max(s, axis=-1, keepdims=True)
                e = jnp.exp2((s - peak) * EXP_SCALE)
                total = jnp.sum(e, axis=-1, keepdims=True)
                probs.append((e * (1.0 / total)).astype(jnp.bfloat16).reshape(128, 256))
            for g in range(4):
                lanes = slice(256 * g, 256 * g + 256)
                vv = vbuf[pl.ds(r0, 8), kcols, lanes].reshape(256, 256)
                o = jnp.dot(probs[g], vv, preferred_element_type=jnp.float32)
                o = jnp.where(
                    head_of == 0, o[0:32],
                    jnp.where(head_of == 1, o[32:64],
                              jnp.where(head_of == 2, o[64:96], o[96:128])))
                att[:, cols, lanes] = o.astype(jnp.bfloat16).reshape(2, 16, 256)
            return c2

        lax.fori_loop(0, 5, col_tile, 0)

        x = att[...].reshape(2 * CW, D)
        for n in range(4):
            y = jnp.dot(x, w4[3, :, 256 * n:256 * n + 256], preferred_element_type=jnp.float32)
            for m in range(2):
                dst = 2 * n + m
                slab = win[dst, pl.ds(4 + r0, 2), 16:96, :].astype(jnp.float32)
                res = slab + y[:, CH * m:CH * m + CH].reshape(2, CW, CH)
                ob[dst, pl.ds(r0, 2)] = res.astype(jnp.bfloat16)
        r_local(i).start()
        for k in range(1, NH):
            r_copy(i, k, h, (h + k) % NH).start()
        return carry

    lax.fori_loop(0, ROWS // 2, row_pair, 0)

    def drain(i, carry):
        r_local(i).wait()
        for k in range(1, NH):
            r_copy(i, k, h, (h + k) % NH).wait_send()
            r_copy(i, k, (h + NH - k) % NH, h).wait_recv()
        return carry

    for k in range(1, NH):
        ht = (h + k) % NH
        w_copy(k, h, ht).wait_send()
        o_copy(k, h, ht).wait_send()
        c_copy(k, h, ht).wait_send()
        m_copy(k, h, ht).wait_send()
    for k in range(NH):
        hs = (h + NH - k) % NH

        @pl.when(not_top)
        def _():
            u_copy(k, hs).wait_send()

        @pl.when(not_bot)
        def _():
            d_copy(k, hs).wait_send()
    y_copy(0, yrow, core, y_up).wait_send()
    y_copy(1, yrow, core, y_dn).wait_send()
    y_copy(2, yrow, core, sib).wait_send()
    y_copy(3, y1, core, y_up, 0, half).wait_send()
    y_copy(4, y3, core, y_dn, half, half).wait_send()
    y_copy(5, y1, core, sib).wait_send()
    y_copy(6, y3, core, sib).wait_send()
    y_copy(7, y2, core, sib).wait_send()
    lax.fori_loop(0, ROWS // 2, drain, 0)


def per_device(cells, conv_weight, qkv_weight, out_weight, block_mask):
    hbm = pl.BlockSpec(memory_space=pl.ANY)
    bf = jnp.bfloat16
    sem = pltpu.SemaphoreType.DMA
    pairs = ROWS // 2
    return pl.pallas_call(
        kernel,
        out_shape=jax.ShapeDtypeStruct((1, ROWS, COLS, CH), bf),
        in_specs=[hbm, hbm, hbm, hbm, pl.BlockSpec(memory_space=pltpu.SMEM)],
        out_specs=hbm,
        scratch_shapes=[
            pltpu.VMEM((NH, WROWS, BC, CH), bf),
            pltpu.VMEM((4, D, D), bf),
            pltpu.VMEM((NH, 9, CH), jnp.float32),
            pltpu.VMEM((KROWS * WC, D), bf),
            pltpu.VMEM((ROWS, CW, D), bf),
            pltpu.VMEM((KROWS, WC, D), bf),
            pltpu.VMEM((KROWS, WC, D), bf),
            pltpu.VMEM((2, CW, D), bf),
            pltpu.VMEM((NH, ROWS, CW, CH), bf),
            sem((4,)),
            sem((NH,)), sem((NH,)), sem((NH,)), sem((NH,)), sem((NH,)), sem((NH,)),
            sem((NH,)), sem((NH,)), sem((NH,)), sem((NH,)), sem((NH,)), sem((NH,)),
            sem((8,)), sem((8,)),
            sem((pairs, NH)), sem((pairs, NH)), sem((pairs,)),
        ],
        compiler_params=pltpu.CompilerParams(
            collective_id=0, has_side_effects=True, vmem_limit_bytes=56 * 1024 * 1024),
        name="band_layer",
    )(cells, conv_weight, qkv_weight, out_weight, block_mask)


def solution(mesh):
    placed = (
        P("tile", None, None, "head"),
        P(None, "head"),
        P(None, None, "head"),
        P(None, "head"),
        P(),
    )
    return jax.shard_map(
        per_device,
        mesh=mesh,
        in_specs=placed,
        out_specs=P("tile", None, None, "head"),
        check_vma=False,
    )
```

```python
import functools
import math

import jax
import jax.numpy as jnp
from jax import lax
from jax.experimental import pallas as pl
from jax.experimental.pallas import tpu as pltpu
from jax.sharding import PartitionSpec as P

MESH = pl.DeviceIdType.MESH
NT = 16
NH = 8
ROWS = 12
COLS = 640
CW = 80
WC = 96
BC = 112
CH = 128
D = 1024
TILE = 32
WROWS = ROWS + 8
KROWS = ROWS + 6
SLAB = 128
AHEAD = 2
EARLY = 4
NEG = -1e30
EXP_SCALE = math.log2(math.e) / 8.0


def kernel(
    cells, conv_w, wqkv, wout, bmask, out,
    win, w4, cw, mixed, qbuf, kbuf, vbuf, att, ob,
    loc_sem, w_s, w_r, o_s, o_r, c_s, c_r, m_s, m_r, u_s, u_r, d_s, d_r,
    y_s, y_r, r_s, r_r,
):
    t = lax.axis_index("tile")
    h = lax.axis_index("head")
    yrow = t // 4
    core = t % 2
    low = (t // 2) % 2
    y_up = (t + 4) % NT
    y_dn = (t + 12) % NT
    sib = t + 1 - 2 * core
    flip = 2 - 4 * low
    tc = t + flip
    not_top = tc > 0
    not_bot = tc < NT - 1

    def place_of(b):
        return b + 2 - 4 * ((b // 2) % 2)

    above = place_of((tc + NT - 1) % NT)
    below = place_of((tc + 1) % NT)

    def slab_row(yy, cc):
        return pl.multiple_of(SLAB * (2 * yy + cc), SLAB)

    @pl.when(tc == 0)
    def _():
        win[:, 0:4] = jnp.zeros((NH, 4, BC, CH), jnp.bfloat16)

    @pl.when(tc == NT - 1)
    def _():
        win[:, 16:20] = jnp.zeros((NH, 4, BC, CH), jnp.bfloat16)

    @pl.when(h == 0)
    def _():
        win[:, :, 0:16] = jnp.zeros((NH, WROWS, 16, CH), jnp.bfloat16)

    @pl.when(h == NH - 1)
    def _():
        win[:, :, 96:112] = jnp.zeros((NH, WROWS, 16, CH), jnp.bfloat16)

    bar = pltpu.get_barrier_semaphore()
    for k in range(1, NH):
        pl.semaphore_signal(bar, inc=1, device_id=(t, (h + k) % NH), device_id_type=MESH)
    for other in (y_up, y_dn):
        pl.semaphore_signal(bar, inc=1, device_id=(other, h), device_id_type=MESH)
    for k in range(NH):
        pl.semaphore_signal(bar, inc=1, device_id=(tc, (h + k) % NH), device_id_type=MESH)

    @pl.when(not_top)
    def _():
        pl.semaphore_signal(bar, inc=1, device_id=(above, h), device_id_type=MESH)

    @pl.when(not_bot)
    def _():
        pl.semaphore_signal(bar, inc=1, device_id=(below, h), device_id_type=MESH)

    bands_near = jnp.where(not_top, 1, 0) + jnp.where(not_bot, 1, 0)
    pl.semaphore_wait(bar, NH - 1 + 2 + NH + bands_near)

    def win_start(hd):
        return pl.multiple_of(jnp.clip(CW * hd - 8, 0, COLS - WC), 8)

    def win_at(hd):
        return pl.multiple_of(win_start(hd) - CW * hd + 16, 8)

    own_rows = slab_row(yrow, core)

    def tile_for(hs, ht):
        return t + flip * ((hs // 4 + ht // 4) % 2)

    def w_copy(k, hs, ht):
        return pltpu.make_async_remote_copy(
            src_ref=wqkv.at[:, pl.ds(own_rows, SLAB), :],
            dst_ref=w4.at[0:3, pl.ds(own_rows, SLAB), pl.ds(pl.multiple_of(CH * hs, CH), CH)],
            send_sem=w_s.at[k], recv_sem=w_r.at[k],
            device_id=(tile_for(hs, ht), ht), device_id_type=MESH)

    def o_copy(k, hs, ht):
        return pltpu.make_async_remote_copy(
            src_ref=wout.at[pl.ds(own_rows, SLAB), :],
            dst_ref=w4.at[3, pl.ds(own_rows, SLAB), pl.ds(pl.multiple_of(CH * hs, CH), CH)],
            send_sem=o_s.at[k], recv_sem=o_r.at[k],
            device_id=(tile_for(hs, ht), ht), device_id_type=MESH)

    def c_copy(k, hs, ht):
        return pltpu.make_async_remote_copy(
            src_ref=conv_w, dst_ref=cw.at[hs],
            send_sem=c_s.at[k], recv_sem=c_r.at[k],
            device_id=(t, ht), device_id_type=MESH)

    def m_copy(k, hs, ht):
        return pltpu.make_async_remote_copy(
            src_ref=cells.at[0, :, pl.ds(win_start(ht), WC), :],
            dst_ref=win.at[hs, 4:16, pl.ds(win_at(ht), WC), :],
            send_sem=m_s.at[k], recv_sem=m_r.at[k],
            device_id=(tc, ht), device_id_type=MESH)

    own_win = pl.ds(win_at(h), WC)

    def u_copy(k, hs):
        return pltpu.make_async_remote_copy(
            src_ref=win.at[hs, 4:8, own_win, :], dst_ref=win.at[hs, 16:20, own_win, :],
            send_sem=u_s.at[k], recv_sem=u_r.at[k],
            device_id=(above, h), device_id_type=MESH)

    def d_copy(k, hs):
        return pltpu.make_async_remote_copy(
            src_ref=win.at[hs, 12:16, own_win, :], dst_ref=win.at[hs, 0:4, own_win, :],
            send_sem=d_s.at[k], recv_sem=d_r.at[k],
            device_id=(below, h), device_id_type=MESH)

    def pass_on(k):
        hs = (h + NH - k) % NH

        @pl.when(not_top)
        def _():
            u_copy(k, hs).start()

        @pl.when(not_bot)
        def _():
            d_copy(k, hs).start()

    local = [
        pltpu.make_async_copy(
            wqkv.at[:, pl.ds(own_rows, SLAB), :],
            w4.at[0:3, pl.ds(own_rows, SLAB), pl.ds(pl.multiple_of(CH * h, CH), CH)], loc_sem.at[0]),
        pltpu.make_async_copy(
            wout.at[pl.ds(own_rows, SLAB), :],
            w4.at[3, pl.ds(own_rows, SLAB), pl.ds(pl.multiple_of(CH * h, CH), CH)], loc_sem.at[1]),
        pltpu.make_async_copy(conv_w, cw.at[h], loc_sem.at[2]),
    ]
    for k in range(1, NH):
        ht = (h + k) % NH
        w_copy(k, h, ht).start()
        o_copy(k, h, ht).start()
    for cp in local:
        cp.start()
    for k in range(1, NH):
        c_copy(k, h, (h + k) % NH).start()
    for k in range(NH):
        m_copy(k, h, (h + k) % NH).start()

    def y_copy(idx, yy, cc, to, first=0, size=SLAB):
        rows = pl.ds(pl.multiple_of(slab_row(yy, cc) + first, size), size)
        return pltpu.make_async_remote_copy(
            src_ref=w4.at[:, rows, :], dst_ref=w4.at[:, rows, :],
            send_sem=y_s.at[idx], recv_sem=y_r.at[idx],
            device_id=(to, h), device_id_type=MESH)

    y1 = (yrow + 3) % 4
    y2 = (yrow + 2) % 4
    y3 = (yrow + 1) % 4
    other = 1 - core
    half = SLAB // 2

    local[0].wait()
    local[1].wait()
    for k in range(1, NH):
        hs = (h + NH - k) % NH
        w_copy(k, hs, h).wait_recv()
        o_copy(k, hs, h).wait_recv()
    y_copy(0, yrow, core, y_up).start()
    y_copy(1, yrow, core, y_dn).start()
    y_copy(2, yrow, core, sib).start()

    local[2].wait()
    for k in range(AHEAD):
        m_copy(k, (h + NH - k) % NH, h).wait_recv()
        pass_on(k)

    def conv_chunk(k, carry):
        hs = (h + NH - k) % NH

        @pl.when(k + AHEAD < NH)
        def _():
            m_copy(k + AHEAD, (hs + NH - AHEAD) % NH, h).wait_recv()
            pass_on(k + AHEAD)

        @pl.when(k > 0)
        def _():
            c_copy(k, hs, h).wait_recv()

        @pl.when(not_bot)
        def _():
            u_copy(k, hs).wait_recv()

        @pl.when(not_top)
        def _():
            d_copy(k, hs).wait_recv()

        taps = [jnp.broadcast_to(cw[hs, pl.ds(i, 1), :], (WC, CH)) for i in range(9)]
        lanes = pl.ds(pl.multiple_of(CH * hs, CH), CH)

        def row(i):
            return win[hs, i].astype(jnp.float32)[8:104]

        rows = [row(0), row(1), None]
        for r in range(KROWS):
            rows[2] = row(r + 2)
            side = []
            for b in range(3):
                acc = taps[b] * rows[0]
                acc = acc + taps[3 + b] * rows[1]
                acc = acc + taps[6 + b] * rows[2]
                side.append(acc)
            conv = pltpu.roll(side[0], 1, 0) + side[1] + pltpu.roll(side[2], WC - 1, 0)
            mixed[pl.ds(WC * r, WC), lanes] = (rows[1] + conv).astype(jnp.bfloat16)
            rows = [rows[1], rows[2], None]
        return carry

    lax.fori_loop(0, EARLY, conv_chunk, 0)

    y_copy(0, y1, core, y_up).wait_recv()
    y_copy(3, y1, core, y_up, 0, half).start()
    y_copy(5, y1, core, sib).start()
    y_copy(1, y3, core, y_dn).wait_recv()
    y_copy(4, y3, core, y_dn, half, half).start()
    y_copy(6, y3, core, sib).start()

    lax.fori_loop(EARLY, NH, conv_chunk, 0)

    y_copy(3, y2, core, y_up, 0, half).wait_recv()
    y_copy(4, y2, core, y_dn, half, half).wait_recv()
    y_copy(7, y2, core, sib).start()

    y_copy(2, yrow, other, sib).wait_recv()
    y_copy(5, y1, other, sib).wait_recv()
    y_copy(6, y3, other, sib).wait_recv()
    y_copy(7, y2, other, sib).wait_recv()

    BLK = 3 * WC

    def kv_block(i, carry):
        def part(n, c2):
            lanes = pl.ds(pl.multiple_of(256 * n, 256), 256)
            x = mixed[pl.ds(pl.multiple_of(BLK * i, BLK), BLK), :]
            for plane, ref in ((1, kbuf), (2, vbuf)):
                y = jnp.dot(x, w4[plane, :, lanes], preferred_element_type=jnp.float32)
                ref[pl.ds(3 * i, 3), :, lanes] = y.astype(jnp.bfloat16).reshape(3, WC, 256)
            return c2

        return lax.fori_loop(0, 4, part, carry)

    def q_block(i, carry):
        def part(n, c2):
            lanes = pl.ds(pl.multiple_of(256 * n, 256), 256)
            x = mixed[pl.ds(pl.multiple_of(BLK * (i + 1), BLK), BLK), :]
            y = jnp.dot(x, w4[0, :, lanes], preferred_element_type=jnp.float32)
            y = y.reshape(3, WC, 256)[:, 8:88]
            qbuf[pl.ds(3 * i, 3), :, lanes] = y.astype(jnp.bfloat16)
            return c2

        return lax.fori_loop(0, 4, part, carry)

    lax.fori_loop(0, 6, kv_block, 0)
    lax.fori_loop(0, 4, q_block, 0)

    qi = lax.broadcasted_iota(jnp.int32, (32, 256), 0)
    ki = lax.broadcasted_iota(jnp.int32, (32, 256), 1)
    drow = ki // 32 - qi // 16 - 3
    dcol = ki % 32 - qi % 16 - 8
    band = (drow >= -3) & (drow <= 3) & (dcol >= -3) & (dcol <= 3)
    self_bias = jnp.where((drow == 0) & (dcol == 0), 0.0, NEG).astype(jnp.float32)
    band_f = jnp.where(band, 1.0, 0.0).astype(jnp.float32)
    lane1 = lax.broadcasted_iota(jnp.int32, (1, 256), 1)
    head_of = lax.broadcasted_iota(jnp.int32, (32, 256), 1) // 64
    head_on = [jnp.where(head_of == i, 1.0, 0.0).astype(jnp.bfloat16) for i in range(4)]

    def occ_at(rt, ct):
        inside = (rt >= 0) & (rt < 6) & (ct >= 0) & (ct < 20)
        value = bmask[jnp.clip(rt, 0, 5), jnp.clip(ct, 0, 19)]
        return jnp.where(inside, value, 0)

    def r_copy(i, k, hs, ht):
        return pltpu.make_async_remote_copy(
            src_ref=ob.at[ht, pl.ds(2 * i, 2)],
            dst_ref=out.at[0, pl.ds(2 * i, 2), pl.ds(pl.multiple_of(CW * hs, 16), CW), :],
            send_sem=r_s.at[i, k], recv_sem=r_r.at[i, k],
            device_id=(tc, ht), device_id_type=MESH)

    def row_pair(i, carry):
        r0 = 2 * i

        def col_tile(j, c2):
            row0 = ROWS * tc - 3 + r0
            col0 = CW * h - 8 + 16 * j
            rt = (row0 + 32) // 32 - 1
            ct = (col0 + 32) // 32 - 1
            in_r = (row0 + lane1 // 32 + 32) // 32 - 1 == rt
            in_c = (col0 + lane1 % 32 + 32) // 32 - 1 == ct
            occ = jnp.where(
                in_r,
                jnp.where(in_c, occ_at(rt, ct), occ_at(rt, ct + 1)),
                jnp.where(in_c, occ_at(rt + 1, ct), occ_at(rt + 1, ct + 1)))
            occ_f = occ.astype(jnp.float32)
            bias = jnp.where(band_f * occ_f > 0.5, 0.0, self_bias)
            cols = pl.ds(pl.multiple_of(16 * j, 16), 16)
            kcols = pl.ds(pl.multiple_of(16 * j, 16), 32)
            scores, probs = [], []
            for g in range(4):
                lanes = slice(256 * g, 256 * g + 256)
                q = qbuf[pl.ds(r0, 2), cols, lanes].reshape(32, 256)
                kk = kbuf[pl.ds(r0, 8), kcols, lanes].reshape(256, 256)
                q4 = jnp.concatenate([q * head_on[n] for n in range(4)], axis=0)
                scores.append(lax.dot_general(q4, kk, (((1,), (1,)), ((), ())),
                                              preferred_element_type=jnp.float32))
            for g in range(4):
                s = scores[g].reshape(4, 32, 256) + bias[None]
                peak = jnp.max(s, axis=-1, keepdims=True)
                e = jnp.exp2((s - peak) * EXP_SCALE)
                total = jnp.sum(e, axis=-1, keepdims=True)
                probs.append((e * (1.0 / total)).astype(jnp.bfloat16).reshape(128, 256))
            for g in range(4):
                lanes = slice(256 * g, 256 * g + 256)
                vv = vbuf[pl.ds(r0, 8), kcols, lanes].reshape(256, 256)
                o = jnp.dot(probs[g], vv, preferred_element_type=jnp.float32)
                o = jnp.where(
                    head_of == 0, o[0:32],
                    jnp.where(head_of == 1, o[32:64],
                              jnp.where(head_of == 2, o[64:96], o[96:128])))
                att[:, cols, lanes] = o.astype(jnp.bfloat16).reshape(2, 16, 256)
            return c2

        lax.fori_loop(0, 5, col_tile, 0)

        x = att[...].reshape(2 * CW, D)
        for n in range(4):
            y = jnp.dot(x, w4[3, :, 256 * n:256 * n + 256], preferred_element_type=jnp.float32)
            for m in range(2):
                dst = 2 * n + m
                slab = win[dst, pl.ds(4 + r0, 2), 16:96, :].astype(jnp.float32)
                res = slab + y[:, CH * m:CH * m + CH].reshape(2, CW, CH)
                ob[dst, pl.ds(r0, 2)] = res.astype(jnp.bfloat16)
        for k in range(NH):
            r_copy(i, k, h, (h + k) % NH).start()
        return carry

    lax.fori_loop(0, ROWS // 2, row_pair, 0)

    def drain(i, carry):
        for k in range(NH):
            r_copy(i, k, h, (h + k) % NH).wait_send()
            r_copy(i, k, (h + NH - k) % NH, h).wait_recv()
        return carry

    for k in range(1, NH):
        ht = (h + k) % NH
        w_copy(k, h, ht).wait_send()
        o_copy(k, h, ht).wait_send()
        c_copy(k, h, ht).wait_send()
    for k in range(NH):
        hs = (h + NH - k) % NH
        m_copy(k, h, (h + k) % NH).wait_send()

        @pl.when(not_top)
        def _():
            u_copy(k, hs).wait_send()

        @pl.when(not_bot)
        def _():
            d_copy(k, hs).wait_send()
    y_copy(0, yrow, core, y_up).wait_send()
    y_copy(1, yrow, core, y_dn).wait_send()
    y_copy(2, yrow, core, sib).wait_send()
    y_copy(3, y1, core, y_up, 0, half).wait_send()
    y_copy(4, y3, core, y_dn, half, half).wait_send()
    y_copy(5, y1, core, sib).wait_send()
    y_copy(6, y3, core, sib).wait_send()
    y_copy(7, y2, core, sib).wait_send()
    lax.fori_loop(0, ROWS // 2, drain, 0)


def per_device(cells, conv_weight, qkv_weight, out_weight, block_mask):
    hbm = pl.BlockSpec(memory_space=pl.ANY)
    bf = jnp.bfloat16
    sem = pltpu.SemaphoreType.DMA
    pairs = ROWS // 2
    return pl.pallas_call(
        kernel,
        out_shape=jax.ShapeDtypeStruct((1, ROWS, COLS, CH), bf),
        in_specs=[hbm, hbm, hbm, hbm, pl.BlockSpec(memory_space=pltpu.SMEM)],
        out_specs=hbm,
        scratch_shapes=[
            pltpu.VMEM((NH, WROWS, BC, CH), bf),
            pltpu.VMEM((4, D, D), bf),
            pltpu.VMEM((NH, 9, CH), jnp.float32),
            pltpu.VMEM((KROWS * WC, D), bf),
            pltpu.VMEM((ROWS, CW, D), bf),
            pltpu.VMEM((KROWS, WC, D), bf),
            pltpu.VMEM((KROWS, WC, D), bf),
            pltpu.VMEM((2, CW, D), bf),
            pltpu.VMEM((NH, ROWS, CW, CH), bf),
            sem((3,)),
            sem((NH,)), sem((NH,)), sem((NH,)), sem((NH,)), sem((NH,)), sem((NH,)),
            sem((NH,)), sem((NH,)), sem((NH,)), sem((NH,)), sem((NH,)), sem((NH,)),
            sem((8,)), sem((8,)),
            sem((pairs, NH)), sem((pairs, NH)),
        ],
        compiler_params=pltpu.CompilerParams(
            collective_id=0, has_side_effects=True, vmem_limit_bytes=56 * 1024 * 1024),
        name="band_layer",
    )(cells, conv_weight, qkv_weight, out_weight, block_mask)


def solution(mesh):
    placed = (
        P("tile", None, None, "head"),
        P(None, "head"),
        P(None, None, "head"),
        P(None, "head"),
        P(),
    )
    return jax.shard_map(
        per_device,
        mesh=mesh,
        in_specs=placed,
        out_specs=P("tile", None, None, "head"),
        check_vma=False,
    )
```

```python
import functools
import math

import jax
import jax.numpy as jnp
from jax import lax
from jax.experimental import pallas as pl
from jax.experimental.pallas import tpu as pltpu
from jax.sharding import PartitionSpec as P

MESH = pl.DeviceIdType.MESH
NT = 16
NH = 8
ROWS = 12
COLS = 640
CW = 80
WC = 96
BC = 112
CH = 128
D = 1024
TILE = 32
WROWS = ROWS + 8
KROWS = ROWS + 6
SLAB = 128
AHEAD = 4
EARLY = 1
NEG = -1e30
EXP_SCALE = math.log2(math.e) / 8.0


def kernel(
    cells, conv_w, wqkv, wout, bmask, out,
    win, w4, cw, mixed, qbuf, kbuf, vbuf, att, ob,
    loc_sem, w_s, w_r, o_s, o_r, c_s, c_r, m_s, m_r, u_s, u_r, d_s, d_r,
    y_s, y_r, r_s, r_r,
):
    t = lax.axis_index("tile")
    h = lax.axis_index("head")
    yrow = t // 4
    core = t % 2
    low = (t // 2) % 2
    y_up = (t + 4) % NT
    y_dn = (t + 12) % NT
    sib = t + 1 - 2 * core
    flip = 2 - 4 * low
    tc = t + flip
    not_top = tc > 0
    not_bot = tc < NT - 1

    def place_of(b):
        return b + 2 - 4 * ((b // 2) % 2)

    above = place_of((tc + NT - 1) % NT)
    below = place_of((tc + 1) % NT)

    def slab_row(yy, cc):
        return pl.multiple_of(SLAB * (2 * yy + cc), SLAB)

    @pl.when(tc == 0)
    def _():
        win[:, 0:4] = jnp.zeros((NH, 4, BC, CH), jnp.bfloat16)

    @pl.when(tc == NT - 1)
    def _():
        win[:, 16:20] = jnp.zeros((NH, 4, BC, CH), jnp.bfloat16)

    @pl.when(h == 0)
    def _():
        win[:, :, 0:16] = jnp.zeros((NH, WROWS, 16, CH), jnp.bfloat16)

    @pl.when(h == NH - 1)
    def _():
        win[:, :, 96:112] = jnp.zeros((NH, WROWS, 16, CH), jnp.bfloat16)

    bar = pltpu.get_barrier_semaphore()
    for k in range(1, NH):
        pl.semaphore_signal(bar, inc=1, device_id=(t, (h + k) % NH), device_id_type=MESH)
    for other in (y_up, y_dn):
        pl.semaphore_signal(bar, inc=1, device_id=(other, h), device_id_type=MESH)
    for k in range(NH):
        pl.semaphore_signal(bar, inc=1, device_id=(tc, (h + k) % NH), device_id_type=MESH)

    @pl.when(not_top)
    def _():
        pl.semaphore_signal(bar, inc=1, device_id=(above, h), device_id_type=MESH)

    @pl.when(not_bot)
    def _():
        pl.semaphore_signal(bar, inc=1, device_id=(below, h), device_id_type=MESH)

    bands_near = jnp.where(not_top, 1, 0) + jnp.where(not_bot, 1, 0)
    pl.semaphore_wait(bar, NH - 1 + 2 + NH + bands_near)

    def win_start(hd):
        return pl.multiple_of(jnp.clip(CW * hd - 8, 0, COLS - WC), 8)

    def win_at(hd):
        return pl.multiple_of(win_start(hd) - CW * hd + 16, 8)

    own_rows = slab_row(yrow, core)

    def tile_for(hs, ht):
        return t + flip * ((hs // 4 + ht // 4) % 2)

    def w_copy(k, hs, ht):
        return pltpu.make_async_remote_copy(
            src_ref=wqkv.at[:, pl.ds(own_rows, SLAB), :],
            dst_ref=w4.at[0:3, pl.ds(own_rows, SLAB), pl.ds(pl.multiple_of(CH * hs, CH), CH)],
            send_sem=w_s.at[k], recv_sem=w_r.at[k],
            device_id=(tile_for(hs, ht), ht), device_id_type=MESH)

    def o_copy(k, hs, ht):
        return pltpu.make_async_remote_copy(
            src_ref=wout.at[pl.ds(own_rows, SLAB), :],
            dst_ref=w4.at[3, pl.ds(own_rows, SLAB), pl.ds(pl.multiple_of(CH * hs, CH), CH)],
            send_sem=o_s.at[k], recv_sem=o_r.at[k],
            device_id=(tile_for(hs, ht), ht), device_id_type=MESH)

    def c_copy(k, hs, ht):
        return pltpu.make_async_remote_copy(
            src_ref=conv_w, dst_ref=cw.at[hs],
            send_sem=c_s.at[k], recv_sem=c_r.at[k],
            device_id=(t, ht), device_id_type=MESH)

    def m_copy(k, hs, ht):
        return pltpu.make_async_remote_copy(
            src_ref=cells.at[0, :, pl.ds(win_start(ht), WC), :],
            dst_ref=win.at[hs, 4:16, pl.ds(win_at(ht), WC), :],
            send_sem=m_s.at[k], recv_sem=m_r.at[k],
            device_id=(tc, ht), device_id_type=MESH)

    own_win = pl.ds(win_at(h), WC)

    def u_copy(k, hs):
        return pltpu.make_async_remote_copy(
            src_ref=win.at[hs, 4:8, own_win, :], dst_ref=win.at[hs, 16:20, own_win, :],
            send_sem=u_s.at[k], recv_sem=u_r.at[k],
            device_id=(above, h), device_id_type=MESH)

    def d_copy(k, hs):
        return pltpu.make_async_remote_copy(
            src_ref=win.at[hs, 12:16, own_win, :], dst_ref=win.at[hs, 0:4, own_win, :],
            send_sem=d_s.at[k], recv_sem=d_r.at[k],
            device_id=(below, h), device_id_type=MESH)

    def pass_on(k):
        hs = (h + NH - k) % NH

        @pl.when(not_top)
        def _():
            u_copy(k, hs).start()

        @pl.when(not_bot)
        def _():
            d_copy(k, hs).start()

    local = [
        pltpu.make_async_copy(
            wqkv.at[:, pl.ds(own_rows, SLAB), :],
            w4.at[0:3, pl.ds(own_rows, SLAB), pl.ds(pl.multiple_of(CH * h, CH), CH)], loc_sem.at[0]),
        pltpu.make_async_copy(
            wout.at[pl.ds(own_rows, SLAB), :],
            w4.at[3, pl.ds(own_rows, SLAB), pl.ds(pl.multiple_of(CH * h, CH), CH)], loc_sem.at[1]),
        pltpu.make_async_copy(conv_w, cw.at[h], loc_sem.at[2]),
    ]
    for k in range(1, NH):
        ht = (h + k) % NH
        w_copy(k, h, ht).start()
        o_copy(k, h, ht).start()
    for cp in local:
        cp.start()
    for k in range(1, NH):
        c_copy(k, h, (h + k) % NH).start()
    for k in range(NH):
        m_copy(k, h, (h + k) % NH).start()

    def y_copy(idx, yy, cc, to, first=0, size=SLAB):
        rows = pl.ds(pl.multiple_of(slab_row(yy, cc) + first, size), size)
        return pltpu.make_async_remote_copy(
            src_ref=w4.at[:, rows, :], dst_ref=w4.at[:, rows, :],
            send_sem=y_s.at[idx], recv_sem=y_r.at[idx],
            device_id=(to, h), device_id_type=MESH)

    y1 = (yrow + 3) % 4
    y2 = (yrow + 2) % 4
    y3 = (yrow + 1) % 4
    other = 1 - core
    half = SLAB // 2

    local[0].wait()
    local[1].wait()
    for k in range(1, NH):
        hs = (h + NH - k) % NH
        w_copy(k, hs, h).wait_recv()
        o_copy(k, hs, h).wait_recv()
    y_copy(0, yrow, core, y_up).start()
    y_copy(1, yrow, core, y_dn).start()
    y_copy(2, yrow, core, sib).start()

    local[2].wait()
    for k in range(AHEAD):
        m_copy(k, (h + NH - k) % NH, h).wait_recv()
        pass_on(k)

    def conv_chunk(k, carry):
        hs = (h + NH - k) % NH

        @pl.when(k + AHEAD < NH)
        def _():
            m_copy(k + AHEAD, (hs + NH - AHEAD) % NH, h).wait_recv()
            pass_on(k + AHEAD)

        @pl.when(k > 0)
        def _():
            c_copy(k, hs, h).wait_recv()

        @pl.when(not_bot)
        def _():
            u_copy(k, hs).wait_recv()

        @pl.when(not_top)
        def _():
            d_copy(k, hs).wait_recv()

        taps = [jnp.broadcast_to(cw[hs, pl.ds(i, 1), :], (WC, CH)) for i in range(9)]
        lanes = pl.ds(pl.multiple_of(CH * hs, CH), CH)

        def row(i):
            return win[hs, i].astype(jnp.float32)[8:104]

        rows = [row(0), row(1), None]
        for r in range(KROWS):
            rows[2] = row(r + 2)
            side = []
            for b in range(3):
                acc = taps[b] * rows[0]
                acc = acc + taps[3 + b] * rows[1]
                acc = acc + taps[6 + b] * rows[2]
                side.append(acc)
            conv = pltpu.roll(side[0], 1, 0) + side[1] + pltpu.roll(side[2], WC - 1, 0)
            mixed[pl.ds(WC * r, WC), lanes] = (rows[1] + conv).astype(jnp.bfloat16)
            rows = [rows[1], rows[2], None]
        return carry

    lax.fori_loop(0, EARLY, conv_chunk, 0)

    y_copy(0, y1, core, y_up).wait_recv()
    y_copy(3, y1, core, y_up, 0, half).start()
    y_copy(5, y1, core, sib).start()
    y_copy(1, y3, core, y_dn).wait_recv()
    y_copy(4, y3, core, y_dn, half, half).start()
    y_copy(6, y3, core, sib).start()

    lax.fori_loop(EARLY, NH, conv_chunk, 0)

    y_copy(3, y2, core, y_up, 0, half).wait_recv()
    y_copy(4, y2, core, y_dn, half, half).wait_recv()
    y_copy(7, y2, core, sib).start()

    y_copy(2, yrow, other, sib).wait_recv()
    y_copy(5, y1, other, sib).wait_recv()
    y_copy(6, y3, other, sib).wait_recv()
    y_copy(7, y2, other, sib).wait_recv()

    BLK = 3 * WC

    def kv_block(i, carry):
        def part(n, c2):
            lanes = pl.ds(pl.multiple_of(256 * n, 256), 256)
            x = mixed[pl.ds(pl.multiple_of(BLK * i, BLK), BLK), :]
            for plane, ref in ((1, kbuf), (2, vbuf)):
                y = jnp.dot(x, w4[plane, :, lanes], preferred_element_type=jnp.float32)
                ref[pl.ds(3 * i, 3), :, lanes] = y.astype(jnp.bfloat16).reshape(3, WC, 256)
            return c2

        return lax.fori_loop(0, 4, part, carry)

    def q_block(i, carry):
        def part(n, c2):
            lanes = pl.ds(pl.multiple_of(256 * n, 256), 256)
            x = mixed[pl.ds(pl.multiple_of(BLK * (i + 1), BLK), BLK), :]
            y = jnp.dot(x, w4[0, :, lanes], preferred_element_type=jnp.float32)
            y = y.reshape(3, WC, 256)[:, 8:88]
            qbuf[pl.ds(3 * i, 3), :, lanes] = y.astype(jnp.bfloat16)
            return c2

        return lax.fori_loop(0, 4, part, carry)

    lax.fori_loop(0, 6, kv_block, 0)
    lax.fori_loop(0, 4, q_block, 0)

    qi = lax.broadcasted_iota(jnp.int32, (32, 256), 0)
    ki = lax.broadcasted_iota(jnp.int32, (32, 256), 1)
    drow = ki // 32 - qi // 16 - 3
    dcol = ki % 32 - qi % 16 - 8
    band = (drow >= -3) & (drow <= 3) & (dcol >= -3) & (dcol <= 3)
    self_bias = jnp.where((drow == 0) & (dcol == 0), 0.0, NEG).astype(jnp.float32)
    band_f = jnp.where(band, 1.0, 0.0).astype(jnp.float32)
    lane1 = lax.broadcasted_iota(jnp.int32, (1, 256), 1)
    head_of = lax.broadcasted_iota(jnp.int32, (32, 256), 1) // 64
    head_on = [jnp.where(head_of == i, 1.0, 0.0).astype(jnp.bfloat16) for i in range(4)]

    def occ_at(rt, ct):
        inside = (rt >= 0) & (rt < 6) & (ct >= 0) & (ct < 20)
        value = bmask[jnp.clip(rt, 0, 5), jnp.clip(ct, 0, 19)]
        return jnp.where(inside, value, 0)

    def r_copy(i, k, hs, ht):
        return pltpu.make_async_remote_copy(
            src_ref=ob.at[ht, pl.ds(2 * i, 2)],
            dst_ref=out.at[0, pl.ds(2 * i, 2), pl.ds(pl.multiple_of(CW * hs, 16), CW), :],
            send_sem=r_s.at[i, k], recv_sem=r_r.at[i, k],
            device_id=(tc, ht), device_id_type=MESH)

    def row_pair(i, carry):
        r0 = 2 * i

        def col_tile(j, c2):
            row0 = ROWS * tc - 3 + r0
            col0 = CW * h - 8 + 16 * j
            rt = (row0 + 32) // 32 - 1
            ct = (col0 + 32) // 32 - 1
            in_r = (row0 + lane1 // 32 + 32) // 32 - 1 == rt
            in_c = (col0 + lane1 % 32 + 32) // 32 - 1 == ct
            occ = jnp.where(
                in_r,
                jnp.where(in_c, occ_at(rt, ct), occ_at(rt, ct + 1)),
                jnp.where(in_c, occ_at(rt + 1, ct), occ_at(rt + 1, ct + 1)))
            occ_f = occ.astype(jnp.float32)
            bias = jnp.where(band_f * occ_f > 0.5, 0.0, self_bias)
            cols = pl.ds(pl.multiple_of(16 * j, 16), 16)
            kcols = pl.ds(pl.multiple_of(16 * j, 16), 32)
            scores, probs = [], []
            for g in range(4):
                lanes = slice(256 * g, 256 * g + 256)
                q = qbuf[pl.ds(r0, 2), cols, lanes].reshape(32, 256)
                kk = kbuf[pl.ds(r0, 8), kcols, lanes].reshape(256, 256)
                q4 = jnp.concatenate([q * head_on[n] for n in range(4)], axis=0)
                scores.append(lax.dot_general(q4, kk, (((1,), (1,)), ((), ())),
                                              preferred_element_type=jnp.float32))
            for g in range(4):
                s = scores[g].reshape(4, 32, 256) + bias[None]
                peak = jnp.max(s, axis=-1, keepdims=True)
                e = jnp.exp2((s - peak) * EXP_SCALE)
                total = jnp.sum(e, axis=-1, keepdims=True)
                probs.append((e * (1.0 / total)).astype(jnp.bfloat16).reshape(128, 256))
            for g in range(4):
                lanes = slice(256 * g, 256 * g + 256)
                vv = vbuf[pl.ds(r0, 8), kcols, lanes].reshape(256, 256)
                o = jnp.dot(probs[g], vv, preferred_element_type=jnp.float32)
                o = jnp.where(
                    head_of == 0, o[0:32],
                    jnp.where(head_of == 1, o[32:64],
                              jnp.where(head_of == 2, o[64:96], o[96:128])))
                att[:, cols, lanes] = o.astype(jnp.bfloat16).reshape(2, 16, 256)
            return c2

        lax.fori_loop(0, 5, col_tile, 0)

        x = att[...].reshape(2 * CW, D)
        for n in range(4):
            y = jnp.dot(x, w4[3, :, 256 * n:256 * n + 256], preferred_element_type=jnp.float32)
            for m in range(2):
                dst = 2 * n + m
                slab = win[dst, pl.ds(4 + r0, 2), 16:96, :].astype(jnp.float32)
                res = slab + y[:, CH * m:CH * m + CH].reshape(2, CW, CH)
                ob[dst, pl.ds(r0, 2)] = res.astype(jnp.bfloat16)
        for k in range(NH):
            r_copy(i, k, h, (h + k) % NH).start()
        return carry

    lax.fori_loop(0, ROWS // 2, row_pair, 0)

    def drain(i, carry):
        for k in range(NH):
            r_copy(i, k, h, (h + k) % NH).wait_send()
            r_copy(i, k, (h + NH - k) % NH, h).wait_recv()
        return carry

    for k in range(1, NH):
        ht = (h + k) % NH
        w_copy(k, h, ht).wait_send()
        o_copy(k, h, ht).wait_send()
        c_copy(k, h, ht).wait_send()
    for k in range(NH):
        hs = (h + NH - k) % NH
        m_copy(k, h, (h + k) % NH).wait_send()

        @pl.when(not_top)
        def _():
            u_copy(k, hs).wait_send()

        @pl.when(not_bot)
        def _():
            d_copy(k, hs).wait_send()
    y_copy(0, yrow, core, y_up).wait_send()
    y_copy(1, yrow, core, y_dn).wait_send()
    y_copy(2, yrow, core, sib).wait_send()
    y_copy(3, y1, core, y_up, 0, half).wait_send()
    y_copy(4, y3, core, y_dn, half, half).wait_send()
    y_copy(5, y1, core, sib).wait_send()
    y_copy(6, y3, core, sib).wait_send()
    y_copy(7, y2, core, sib).wait_send()
    lax.fori_loop(0, ROWS // 2, drain, 0)


def per_device(cells, conv_weight, qkv_weight, out_weight, block_mask):
    hbm = pl.BlockSpec(memory_space=pl.ANY)
    bf = jnp.bfloat16
    sem = pltpu.SemaphoreType.DMA
    pairs = ROWS // 2
    return pl.pallas_call(
        kernel,
        out_shape=jax.ShapeDtypeStruct((1, ROWS, COLS, CH), bf),
        in_specs=[hbm, hbm, hbm, hbm, pl.BlockSpec(memory_space=pltpu.SMEM)],
        out_specs=hbm,
        scratch_shapes=[
            pltpu.VMEM((NH, WROWS, BC, CH), bf),
            pltpu.VMEM((4, D, D), bf),
            pltpu.VMEM((NH, 9, CH), jnp.float32),
            pltpu.VMEM((KROWS * WC, D), bf),
            pltpu.VMEM((ROWS, CW, D), bf),
            pltpu.VMEM((KROWS, WC, D), bf),
            pltpu.VMEM((KROWS, WC, D), bf),
            pltpu.VMEM((2, CW, D), bf),
            pltpu.VMEM((NH, ROWS, CW, CH), bf),
            sem((3,)),
            sem((NH,)), sem((NH,)), sem((NH,)), sem((NH,)), sem((NH,)), sem((NH,)),
            sem((NH,)), sem((NH,)), sem((NH,)), sem((NH,)), sem((NH,)), sem((NH,)),
            sem((8,)), sem((8,)),
            sem((pairs, NH)), sem((pairs, NH)),
        ],
        compiler_params=pltpu.CompilerParams(
            collective_id=0, has_side_effects=True, vmem_limit_bytes=56 * 1024 * 1024),
        name="band_layer",
    )(cells, conv_weight, qkv_weight, out_weight, block_mask)


def solution(mesh):
    placed = (
        P("tile", None, None, "head"),
        P(None, "head"),
        P(None, None, "head"),
        P(None, "head"),
        P(),
    )
    return jax.shard_map(
        per_device,
        mesh=mesh,
        in_specs=placed,
        out_specs=P("tile", None, None, "head"),
        check_vma=False,
    )
```
